32 devices in a mesh: dp: 8 (over z, core), seq: 4 (over y, x).
Axes of the slice: x: 2, y: 2, z: 4, core: 2. Of those that a mesh axis runs over, the one named last changes fastest.
Arguments:
- features: bfloat16 [16384, 1536], P(('dp', 'seq')), parts along dimension 0, may hold values from -6 to 6
- conv_taps: float32 [5, 1536], replicated, may hold values from -2.5 to 2.5
- norm_gain: float32 [1536], replicated, may hold values from 0.5 to 2
- point_weight: bfloat16 [1536, 1536], replicated, may hold values from -0.15625 to 0.15625
- donor_weight: bfloat16 [1536, 768], replicated, may hold values from -0.15625 to 0.15625
- accept_weight: bfloat16 [1536, 768], replicated, may hold values from -0.15625 to 0.15625
- donor_pos: int32 [2048], P(('dp', 'seq')), parts along dimension 0, may hold values from 0 to 2047, as said below
- accept_pos: int32 [2048], P(('dp', 'seq')), parts along dimension 0, may hold values from 0 to 2047, as said below
- pair_counts: int32 [32], P(('dp', 'seq')), parts along dimension 0, may hold values from 1 to 64, 128 in all
Outputs:
- encoded: bfloat16 [16384, 1536], P(('dp', 'seq')), parts along dimension 0
- junction: bfloat16 [2048, 768], P(('dp', 'seq')), parts along dimension 0
The draws below stay inside these ranges and needn't reach their ends.
There are 8 independent parts, one for each index of `dp`. The reference program is written for one: setup_inputs(seed, part) draws one part's arguments, and reference() takes and returns one part's arrays. A program takes and returns all parts, laid end to end along the dimension named above; an argument that names none is the same for every part. Nothing has to cross between parts.
Inputs may be any that keep to these rules, and one draw needn't show every extreme that they name: `pair_counts`: the live counts sum to 128 and the largest is exactly 64. `donor_pos`: among the 128 donor and acceptor positions of the slots s * 64 to s * 64 + 63, at most 64 lie in any one block of 512 positions r * 512 to r * 512 + 511, and exactly 64 lie in one such block. `accept_pos`: as for donor_pos, with the two lists counted together.
All inputs are finite; a program needn't handle non-finite values. No bound on the sum of `pair_counts` on one device may be relied on, other than what follows from the above.
Results may differ from the reference program's by a relative error of at most 0.0064.
Values may be sent and summed in bfloat16 or wider, within the bound.
No kernel may reach another device: no remote copies, remote signals or barrier semaphores. Data moves between devices by JAX's collectives and lax.ppermute only.
A program may use at most 128 MiB of HBM per device.

```python
import math
import jax
import jax.numpy as jnp
import numpy as np
from jax import lax

C = 1536
H = 768
TAPS = 5
ROWS = 512
P_DEV = 64
SEQ_LEN = 2048
PAIRS = 256
CAP = 64
N_SEQ = 4


def pair_positions(key):
    base = jax.random.fold_in(key, 7)
    key_full, key_ids, key_mix, key_off = jax.random.split(base, 4)
    count = 2 * P_DEV
    slots_all = N_SEQ * CAP
    full_owner = jax.random.randint(key_full, (N_SEQ,), 0, N_SEQ)
    id_keys = jax.random.split(key_ids, N_SEQ)
    ids = jax.vmap(lambda one: jax.random.permutation(one, slots_all))(id_keys)
    owner_ids = (ids // CAP).astype(jnp.int32)
    order_key = (owner_ids == full_owner[:, None]).astype(jnp.int32) * slots_all + jnp.arange(slots_all, dtype=jnp.int32)[None, :]
    order = jnp.argsort(order_key, axis=1)
    others = jnp.take_along_axis(owner_ids, order, axis=1)[:, :count - CAP]
    owners = jnp.concatenate([jnp.broadcast_to(full_owner[:, None], (N_SEQ, CAP)), others], axis=1)
    mix_keys = jax.random.split(key_mix, N_SEQ)
    mixing = jax.vmap(lambda one: jax.random.permutation(one, count))(mix_keys)
    owners = jnp.take_along_axis(owners, mixing, axis=1)
    offsets = jax.random.randint(key_off, (N_SEQ, count), 0, ROWS)
    positions = (owners * ROWS + offsets).astype(jnp.int32)
    return positions


def draw_donor_pos(key, part):
    return pair_positions(key)[:, :P_DEV].reshape(PAIRS)


def draw_accept_pos(key, part):
    return pair_positions(key)[:, P_DEV:].reshape(PAIRS)


def block_scale(own_key, shape, shards, least, top_value):
    loudness = 1.0
    for position, blocks in shards:
        heights = jax.random.uniform(jax.random.fold_in(jax.random.fold_in(own_key, 6), position), (blocks,), jnp.float32, least / len(shards), top_value / len(shards))
        loudness = loudness * jnp.repeat(jnp.exp(heights), shape[position] // blocks).reshape((-1,) + (1,) * (len(shape) - 1 - position))
    return loudness


def split_up(amount, total, limit, slope):
    weights = [(1 << 20) // math.isqrt(grade ** slope) + 1 for grade in range(2, amount + 1)]
    surplus, holding = total - limit - (amount - 1), [1] * (amount - 1)
    while surplus > 0:
        free = [i for i in range(amount - 1) if holding[i] < limit]
        whole, remaining = sum([weights[i] for i in free]), surplus
        for i in free:
            addition = min(limit - holding[i], max(1, remaining * weights[i] // whole), surplus)
            holding[i] = holding[i] + addition
            surplus = surplus - addition
    return np.array([limit] + holding)


def ragged_sizes(key, amount, total, reach, lean):
    if amount == 2:
        one = jax.random.randint(key, (), max(1, total - reach), min(reach, total - 1) + 1)
        return jnp.stack([one, total - one])
    tallies = jnp.asarray(split_up(amount, total, reach, lean), jnp.int32)
    pairs = (amount - 1) // 2
    source_of, sink = tallies[1:1 + 2 * pairs:2], tallies[2:2 + 2 * pairs:2]
    margin = jnp.minimum(source_of - 1, reach - sink)
    passed = jax.random.randint(jax.random.fold_in(key, 1), (pairs,), 0, 1 << 20) % (margin + 1)
    tallies = tallies.at[1:1 + 2 * pairs:2].set(source_of - passed).at[2:2 + 2 * pairs:2].set(sink + passed)
    return tallies[jax.random.permutation(jax.random.fold_in(key, 2), amount)]


def noise(stream_key, dims, deviation, most, shards=(), kind=jnp.bfloat16):
    loudness = block_scale(stream_key, dims, shards, -0.22, 0.18) if shards else 1.0
    entries = jax.random.normal(stream_key, dims, jnp.float32) * deviation * loudness
    return jnp.minimum(jnp.maximum(entries, -most), most).astype(kind)


def setup_inputs(seed: int = 0, part: int = 0) -> dict:
    arg_keys = jax.random.split(jax.random.key(seed), 10)
    part_splits = jax.random.split(jax.random.fold_in(arg_keys[9], part), 10)
    return {
        "features": noise(part_splits[0], (SEQ_LEN, C), 1.0, 6.0, ((0, 4),)),
        "conv_taps": noise(arg_keys[1], (TAPS, C), TAPS ** -0.5, 2.5, (), jnp.float32),
        "norm_gain": jnp.clip(jnp.exp(jax.random.uniform(arg_keys[2], (C,), jnp.float32, math.log(0.5), math.log(2.0))), 0.5, 2.0),
        "point_weight": noise(arg_keys[3], (C, C), C ** -0.5, 0.15625),
        "donor_weight": noise(arg_keys[4], (C, H), C ** -0.5, 0.15625),
        "accept_weight": noise(arg_keys[5], (C, H), C ** -0.5, 0.15625),
        "donor_pos": draw_donor_pos(jax.random.fold_in(jax.random.fold_in(arg_keys[9], part), 71), part),
        "accept_pos": draw_accept_pos(jax.random.fold_in(jax.random.fold_in(arg_keys[9], part), 71), part),
        "pair_counts": ragged_sizes(part_splits[8], N_SEQ, N_SEQ * P_DEV // 2, P_DEV, 2).astype(jnp.int32),
    }


def reference(features, conv_taps, norm_gain, point_weight, donor_weight, accept_weight, donor_pos, accept_pos, pair_counts):
    padded = jnp.pad(features.astype(jnp.float32), ((2, 2), (0, 0)))
    conv = jnp.zeros((SEQ_LEN, C), jnp.float32)
    for k in range(TAPS):
        conv = conv + conv_taps[k][None, :] * padded[k:k + SEQ_LEN]
    scale = jax.lax.rsqrt(lax.optimization_barrier(jnp.mean(conv * conv, axis=-1, keepdims=True)) + 1e-06)
    normed = (conv * scale * norm_gain[None, :]).astype(jnp.bfloat16)
    mixed = jnp.dot(normed, point_weight, preferred_element_type=jnp.float32)
    encoded = (features.astype(jnp.float32) + jax.nn.gelu(mixed, approximate=False)).astype(jnp.bfloat16)
    donor_rows = jnp.take(encoded, donor_pos.astype(jnp.int32), axis=0)
    accept_rows = jnp.take(encoded, accept_pos.astype(jnp.int32), axis=0)
    slots = jnp.arange(P_DEV, dtype=jnp.int32)[None, :]
    live = (slots < pair_counts.astype(jnp.int32)[:, None]).reshape(PAIRS)
    left = jnp.dot(donor_rows, donor_weight, preferred_element_type=jnp.float32)
    right = jnp.dot(accept_rows, accept_weight, preferred_element_type=jnp.float32)
    junction = jnp.where(live[:, None], jax.nn.silu(left) * right, jnp.float32(0.0)).astype(jnp.bfloat16)
    return (encoded, junction)
```

```python
import functools

import jax
import jax.numpy as jnp
from jax import lax
from jax.experimental import pallas as pl
from jax.experimental.pallas import tpu as pltpu
from jax.sharding import PartitionSpec as P

F32 = jnp.float32
BF16 = jnp.bfloat16
LANES = 128
HALO = 2
MIB = 1 << 20


def vmem(shape, dtype):
    return pltpu.VMEM(shape, dtype)


def whole():
    return pl.BlockSpec(memory_space=pltpu.VMEM)


def far(array):
    return pltpu.with_memory_space_constraint(array, pltpu.MemorySpace.HBM)


def in_hbm():
    return pl.BlockSpec(memory_space=pltpu.MemorySpace.HBM)


def params(mib):
    return pltpu.CompilerParams(vmem_limit_bytes=mib * MIB)


def gelu(v):
    m = jnp.abs(v)
    d = m * F32(0.3275911 * 0.7071067811865476) + F32(1.0)
    u = pl.reciprocal(d, approx=False)
    p = u * F32(0.5 * 1.061405429) + F32(0.5 * -1.453152027)
    p = p * u + F32(0.5 * 1.421413741)
    p = p * u + F32(0.5 * -0.284496736)
    p = p * u + F32(0.5 * 0.254829592)
    e = jnp.exp2(v * v * F32(-0.5 * 1.4426950408889634))
    return jnp.maximum(v, F32(0.0)) - (m * u) * (p * e)


def pack_kernel(feat_hbm, donor_hbm, accept_hbm, count, out_ref, ends, donor, accept, sem):
    channels = out_ref.shape[1]
    rows = feat_hbm.shape[0]
    loads = [
        pltpu.make_async_copy(feat_hbm.at[pl.ds(0, 8)], ends.at[0], sem.at[0]),
        pltpu.make_async_copy(feat_hbm.at[pl.ds(rows - 8, 8)], ends.at[1], sem.at[1]),
        pltpu.make_async_copy(donor_hbm, donor, sem.at[2]),
        pltpu.make_async_copy(accept_hbm, accept, sem.at[3]),
    ]
    for load in loads:
        load.start()
    for load in loads:
        load.wait()
    first = ends[0].astype(F32)
    last = pltpu.roll(ends[1].astype(F32), 2 * HALO, axis=0)
    row = lax.broadcasted_iota(jnp.int32, (8, channels), 0)
    rows = jnp.where(row < HALO, first, jnp.where(row < 2 * HALO, last, F32(0.0)))
    wanted = jnp.concatenate([donor[...], accept[...]], axis=1)
    width = wanted.shape[1]
    live = jnp.full((1, width), count[0], jnp.int32)
    line = jnp.concatenate([wanted >> 8, wanted & 255, live], axis=1).astype(F32)
    spot = lax.broadcasted_iota(jnp.int32, (8, 3 * width), 0) == 2 * HALO
    out_ref[:, 0 : 3 * width] = jnp.where(spot, line, rows[:, 0 : 3 * width]).astype(BF16)
    out_ref[:, 3 * width :] = rows[:, 3 * width :].astype(BF16)


def pack(features, donor, accept, count):
    rows, channels = features.shape
    slots = donor.shape[0]
    return pl.pallas_call(
        pack_kernel,
        in_specs=[in_hbm()] * 3 + [pl.BlockSpec(memory_space=pltpu.SMEM)],
        out_specs=whole(),
        out_shape=vmem((8, channels), BF16),
        scratch_shapes=[
            pltpu.VMEM((2, 8, channels), BF16),
            pltpu.VMEM((1, slots), jnp.int32),
            pltpu.VMEM((1, slots), jnp.int32),
            pltpu.SemaphoreType.DMA((4,)),
        ],
        compiler_params=params(4),
        name="pack",
    )(far(features), far(donor.reshape(1, slots)), far(accept.reshape(1, slots)), count)


def unpack_line(packet_ref, width):
    line = packet_ref[...].astype(F32)[2 * HALO : 2 * HALO + 1, 0 : 3 * width]
    wanted = line[:, 0:width] * F32(256.0) + line[:, width : 2 * width]
    lane = lax.broadcasted_iota(jnp.int32, (1, width), 1)
    slot = jnp.where(lane >= width // 2, lane - width // 2, lane).astype(F32)
    return wanted, slot < line[:, 2 * width :]


def strict_upper(size):
    a = lax.broadcasted_iota(jnp.int32, (size, size), 0)
    b = lax.broadcasted_iota(jnp.int32, (size, size), 1)
    return (a < b).astype(F32).astype(BF16)


def chosen(mine, capacity):
    ranks = jnp.dot(mine.astype(BF16), strict_upper(mine.shape[1]), preferred_element_type=F32)
    keyed = jnp.where(mine > F32(0.5), ranks, F32(-1.0))
    level = lax.broadcasted_iota(jnp.int32, (capacity, mine.shape[1]), 0).astype(F32)
    return lambda k: keyed[k : k + 1, :] == level


def conv_rows(load, taps_ref, gain_ref, columns, eps_scale):
    tap_count = taps_ref.shape[0]
    held = []
    total = None
    for j in range(columns):
        lanes = slice(j * LANES, (j + 1) * LANES)
        acc = None
        for k in range(tap_count):
            term = taps_ref[k : k + 1, lanes] * load(j, k)
            acc = term if acc is None else acc + term
        held.append(acc)
        total = acc * acc if total is None else total + acc * acc
    mean = jnp.sum(total, axis=-1, keepdims=True) * F32(eps_scale)
    scale = lax.rsqrt(mean + F32(1e-06))
    return [
        (held[j] * scale * gain_ref[0:1, j * LANES : (j + 1) * LANES]).astype(BF16)
        for j in range(columns)
    ]


def conv_kernel(
    owners,
    capacity,
    width,
    packet_ref,
    feat_hbm,
    taps_ref,
    gain_ref,
    w_hbm,
    normed_ref,
    feat_ref,
    w_ref,
    spread_ref,
    wide,
    feat_sem,
    weight_sem,
):
    rows, channels = feat_ref.shape
    columns = channels // LANES
    parts = 4
    step = rows // parts
    loads = [
        pltpu.make_async_copy(
            feat_hbm.at[pl.ds(c * step, step)], feat_ref.at[pl.ds(c * step, step)], feat_sem.at[c]
        )
        for c in range(parts)
    ]
    for load in loads:
        load.start()
    weights = [pltpu.make_async_copy(w_hbm, w_ref, weight_sem.at[0])]
    for load in weights:
        load.start()

    me = lax.axis_index("seq")
    wanted, live = unpack_line(packet_ref, width)
    group = lax.broadcasted_iota(jnp.int32, (max(8, owners), width), 0)
    low = ((group ^ me) * rows).astype(F32)
    here = (wanted >= low) & (wanted < low + F32(rows)) & live & (group < owners)
    pick = chosen(jnp.where(here, F32(1.0), F32(0.0)), capacity)
    for k in range(owners):
        spread_ref[k * capacity : (k + 1) * capacity, :] = jnp.where(
            pick(k), F32(1.0), F32(0.0)
        ).astype(BF16)

    edge = jnp.zeros((8, LANES), F32)
    for j in range(columns):
        wide[j, 0:8, :] = edge
        wide[j, rows + 8 : rows + 16, :] = edge

    tile = 32

    def widen(c):
        loads[c].wait()
        for j in range(columns):
            lanes = slice(j * LANES, (j + 1) * LANES)
            wide[j, 8 + c * step : 8 + (c + 1) * step, :] = feat_ref[
                c * step : (c + 1) * step, lanes
            ].astype(F32)

    def convolve(first, count):
        def body(i, carry):
            base = pl.multiple_of(first + i * tile, tile)

            def load(j, k):
                return wide.at[j, pl.ds(base, tile + 16), :][8 - HALO + k : 8 - HALO + k + tile, :]

            out = conv_rows(load, taps_ref, gain_ref, columns, 1.0 / channels)
            for j in range(columns):
                normed_ref[pl.ds(base, tile), j * LANES : (j + 1) * LANES] = out[j]
            return carry

        lax.fori_loop(0, count, body, 0)

    widen(0)
    done = 0
    for c in range(1, parts):
        widen(c)
        ready = c * step // tile * tile
        convolve(done, (ready - done) // tile)
        done = ready
    convolve(done, (rows - done) // tile)
    for load in weights:
        load.wait()


def conv_norm(packet, features, taps, gain, w, owners, capacity, width):
    rows, channels = features.shape
    return pl.pallas_call(
        functools.partial(conv_kernel, owners, capacity, width),
        in_specs=[whole(), in_hbm(), whole(), whole(), in_hbm()],
        out_specs=[whole()] * 4,
        out_shape=[
            vmem((rows, channels), BF16),
            vmem((rows, channels), BF16),
            vmem(w.shape, BF16),
            vmem((owners * capacity, width), BF16),
        ],
        scratch_shapes=[
            pltpu.VMEM((channels // LANES, rows + 16, LANES), F32),
            pltpu.SemaphoreType.DMA((4,)),
            pltpu.SemaphoreType.DMA((1,)),
        ],
        compiler_params=params(6),
        cost_estimate=pl.CostEstimate(flops=30 * rows * channels, bytes_accessed=12 << 20, transcendentals=rows),
        name="conv_norm",
    )(packet, far(features), taps, gain.reshape(1, channels), far(w))


def named_kernel(owners, capacity, width, *refs):
    packets = refs[:owners]
    feat_ref, normed_ref, taps_ref, gain_ref, w_ref, wd_hbm, wa_hbm = refs[owners : owners + 7]
    outs = refs[owners + 7 : 2 * owners + 7]
    patched_ref = refs[2 * owners + 7]
    near, grab, lhs, res, enc, wd_ref, wa_ref, sem = refs[2 * owners + 8 :]
    del normed_ref
    weights = [
        pltpu.make_async_copy(wd_hbm, wd_ref, sem.at[0]),
        pltpu.make_async_copy(wa_hbm, wa_ref, sem.at[1]),
    ]
    for load in weights:
        load.start()
    rows, channels = feat_ref.shape
    columns = channels // LANES
    heads = wd_ref.shape[1]
    me = lax.axis_index("seq")

    above = jnp.zeros((8, channels), F32)
    below = jnp.zeros((8, channels), F32)
    for k in range(1, owners):
        other = packets[k][...].astype(F32)
        above = jnp.where((me ^ k) == me - 1, other, above)
        below = jnp.where((me ^ k) == me + 1, other, below)
    row = lax.broadcasted_iota(jnp.int32, (8, channels), 0)
    above = jnp.where(row >= 8 - HALO, pltpu.roll(above, 8 - 2 * HALO, axis=0), F32(0.0))
    below = jnp.where(row < HALO, below, F32(0.0))
    span = 16
    head = feat_ref[0 : span + 8, :].astype(F32)
    foot = feat_ref[rows - span - 8 : rows, :].astype(F32)
    for j in range(columns):
        lanes = slice(j * LANES, (j + 1) * LANES)
        near[j, 0:8, :] = above[:, lanes]
        near[j, 8 : 16 + span, :] = head[:, lanes]
        near[j, 16 + span : 24 + 2 * span, :] = foot[:, lanes]
        near[j, 24 + 2 * span : 32 + 2 * span, :] = below[:, lanes]
    for origin, place in ((8, 0), (24 + span, rows - span)):

        def load(j, k, origin=origin):
            begin = origin - HALO + k
            return near[j, begin : begin + span, :]

        out = conv_rows(load, taps_ref, gain_ref, columns, 1.0 / channels)
        for j in range(columns):
            patched_ref[place : place + span, j * LANES : (j + 1) * LANES] = out[j]

    groups = max(8, owners)
    group = lax.broadcasted_iota(jnp.int32, (groups, width), 0)
    lane = lax.broadcasted_iota(jnp.int32, (1, width), 1)
    local = jnp.zeros((groups, width), F32)
    mine = jnp.zeros((groups, width), F32)
    start = (me * rows).astype(F32)
    for k in range(owners):
        at, live = unpack_line(packets[k], width)
        at = at - start
        here = (at >= F32(0.0)) & (at < F32(rows)) & live
        mine = jnp.where(group == k, jnp.where(here, F32(1.0), F32(0.0)), mine)
        local = jnp.where(group == k, at, local)
    pick = chosen(mine, capacity)
    mark = F32(1 << 16)
    keyed = local + F32(1.0) + jnp.where(lane >= width // 2, mark, F32(0.0))
    spread = lax.broadcasted_iota(jnp.int32, (capacity, rows), 1).astype(F32)
    kinds = []
    for k in range(owners):
        code = jnp.sum(jnp.where(pick(k), keyed[k : k + 1, :], F32(0.0)), axis=1, keepdims=True)
        accepts = code >= mark
        kinds.append(accepts)
        index = code - jnp.where(accepts, mark, F32(0.0)) - F32(1.0)
        grab[k * capacity : (k + 1) * capacity, :] = jnp.where(
            spread == index, F32(1.0), F32(0.0)
        ).astype(BF16)

    wide = 256
    for j in range(channels // wide):
        lanes = slice(j * wide, (j + 1) * wide)
        lhs[:, lanes] = jnp.dot(
            grab[...], patched_ref[:, lanes], preferred_element_type=F32
        ).astype(BF16)
        res[:, lanes] = jnp.dot(
            grab[...], feat_ref[:, lanes], preferred_element_type=F32
        ).astype(BF16)
    for j in range(channels // wide):
        lanes = slice(j * wide, (j + 1) * wide)
        mixed = jnp.dot(lhs[...], w_ref[:, lanes], preferred_element_type=F32)
        enc[:, lanes] = (res[:, lanes].astype(F32) + gelu(mixed)).astype(BF16)
    for load in weights:
        load.wait()
    for j in range(heads // wide):
        lanes = slice(j * wide, (j + 1) * wide)
        left = jnp.dot(enc[...], wd_ref[:, lanes], preferred_element_type=F32)
        right = jnp.dot(enc[...], wa_ref[:, lanes], preferred_element_type=F32)
        for k in range(owners):
            part = slice(k * capacity, (k + 1) * capacity)
            outs[k][:, lanes] = jnp.where(kinds[k], right[part], left[part]).astype(BF16)


def named(packets, feat, normed, taps, gain, w, wd, wa, width, capacity):
    owners = len(packets)
    rows, channels = feat.shape
    heads = wd.shape[1]
    total = owners * capacity
    out = pl.pallas_call(
        functools.partial(named_kernel, owners, capacity, width),
        in_specs=[whole()] * (owners + 5) + [in_hbm()] * 2,
        out_specs=[whole()] * (owners + 1),
        out_shape=[vmem((capacity, heads), BF16)] * owners + [vmem((rows, channels), BF16)],
        input_output_aliases={owners + 1: owners},
        scratch_shapes=[
            pltpu.VMEM((channels // LANES, 64, LANES), F32),
            pltpu.VMEM((total, rows), BF16),
            pltpu.VMEM((total, channels), BF16),
            pltpu.VMEM((total, channels), BF16),
            pltpu.VMEM((total, channels), BF16),
            pltpu.VMEM(wd.shape, BF16),
            pltpu.VMEM(wa.shape, BF16),
            pltpu.SemaphoreType.DMA((2,)),
        ],
        compiler_params=params(16),
        cost_estimate=pl.CostEstimate(
            flops=4 * total * channels * (channels + rows), bytes_accessed=8 << 20, transcendentals=2 * total * channels
        ),
        name="named_rows",
    )(*packets, feat, normed, taps, gain.reshape(1, channels), w, far(wd), far(wa))
    return out[:owners], out[owners]


def encode_kernel(normed_ref, feat_ref, w_ref, out_hbm, stage, sem):
    rows, channels = feat_ref.shape
    wide = 256
    tall = 256
    copies = []
    for j in range(channels // wide):
        lanes = slice(j * wide, (j + 1) * wide)
        for i in range(rows // tall):
            part = slice(i * tall, (i + 1) * tall)
            mixed = jnp.dot(normed_ref[part, :], w_ref[:, lanes], preferred_element_type=F32)
            stage[part, lanes] = (feat_ref[part, lanes].astype(F32) + gelu(mixed)).astype(BF16)
        copy = pltpu.make_async_copy(
            stage.at[:, pl.ds(j * wide, wide)], out_hbm.at[:, pl.ds(j * wide, wide)], sem.at[j]
        )
        copy.start()
        copies.append(copy)
    for copy in copies:
        copy.wait()


def encode(normed, feat, w):
    rows, channels = feat.shape
    return pl.pallas_call(
        encode_kernel,
        in_specs=[whole()] * 3,
        out_specs=pl.BlockSpec(memory_space=pltpu.MemorySpace.HBM),
        out_shape=jax.ShapeDtypeStruct((rows, channels), BF16),
        scratch_shapes=[pltpu.VMEM((rows, channels), BF16), pltpu.SemaphoreType.DMA((channels // 256,))],
        compiler_params=params(6),
        cost_estimate=pl.CostEstimate(
            flops=2 * rows * channels * channels, bytes_accessed=8 << 20, transcendentals=2 * rows * channels
        ),
        name="encode",
    )(normed, feat, w)


def junction_kernel(owners, *refs):
    blocks = refs[:owners]
    spread_ref, out_ref = refs[owners:]
    slots = out_ref.shape[0]
    capacity = blocks[0].shape[0]
    picked = None
    for k in range(owners):
        part = lax.dot_general(
            spread_ref[k * capacity : (k + 1) * capacity, :],
            blocks[k][...],
            (((0,), (0,)), ((), ())),
            preferred_element_type=F32,
        )
        picked = part if picked is None else picked + part
    left, right = picked[:slots], picked[slots:]
    silu = left / (F32(1.0) + jnp.exp(-left))
    out_ref[...] = (silu * right).astype(BF16)


def junction(blocks, spread):
    slots = spread.shape[1] // 2
    heads = blocks[0].shape[1]
    return pl.pallas_call(
        functools.partial(junction_kernel, len(blocks)),
        in_specs=[whole()] * (len(blocks) + 1),
        out_specs=whole(),
        out_shape=jax.ShapeDtypeStruct((slots, heads), BF16),
        compiler_params=params(6),
        name="junction",
    )(*blocks, spread)


def swap(array, k, owners):
    return lax.ppermute(array, "seq", [(i, i ^ k) for i in range(owners)])


def on_device(
    features,
    conv_taps,
    norm_gain,
    point_weight,
    donor_weight,
    accept_weight,
    donor_pos,
    accept_pos,
    pair_counts,
):
    slots = donor_pos.shape[0]
    owners = lax.axis_size("seq")
    capacity = 2 * ((2 * slots + owners - 1) // owners)
    own = pack(features, donor_pos, accept_pos, pair_counts)
    packets = [own] + [swap(own, k, owners) for k in range(1, owners)]
    width = 2 * slots
    normed, feat, w, spread = conv_norm(
        own, features, conv_taps, norm_gain, point_weight, owners, capacity, width
    )
    sends, patched = named(
        packets, feat, normed, conv_taps, norm_gain, w, donor_weight, accept_weight, width, capacity
    )
    blocks = [sends[0]] + [swap(sends[k], k, owners) for k in range(1, owners)]
    encoded = encode(patched, feat, w)
    return encoded, junction(blocks, spread)


def solution(mesh):
    placed = (
        P(("dp", "seq"), None),
        P(),
        P(),
        P(),
        P(),
        P(),
        P(("dp", "seq")),
        P(("dp", "seq")),
        P(("dp", "seq")),
    )
    return jax.shard_map(
        on_device,
        mesh=mesh,
        in_specs=placed,
        out_specs=(P(("dp", "seq"), None), P(("dp", "seq"), None)),
        check_vma=False,
    )
```

```python
import functools

import jax
import jax.numpy as jnp
from jax import lax
from jax.experimental import pallas as pl
from jax.experimental.pallas import tpu as pltpu
from jax.sharding import PartitionSpec as P


F32 = jnp.float32
BF16 = jnp.bfloat16
LANES = 128
HALO = 2
MIB = 1 << 20


def vmem(shape, dtype):
    return pltpu.VMEM(shape, dtype)


def whole():
    return pl.BlockSpec(memory_space=pltpu.VMEM)


def far(array):
    return pltpu.with_memory_space_constraint(array, pltpu.MemorySpace.HBM)


def in_hbm():
    return pl.BlockSpec(memory_space=pltpu.MemorySpace.HBM)


def params(mib):
    return pltpu.CompilerParams(vmem_limit_bytes=mib * MIB)


def gelu(v):
    m = jnp.abs(v)
    d = m * F32(0.3275911 * 0.7071067811865476) + F32(1.0)
    u = pl.reciprocal(d, approx=False)
    p = u * F32(0.5 * 1.061405429) + F32(0.5 * -1.453152027)
    p = p * u + F32(0.5 * 1.421413741)
    p = p * u + F32(0.5 * -0.284496736)
    p = p * u + F32(0.5 * 0.254829592)
    e = jnp.exp2(v * v * F32(-0.5 * 1.4426950408889634))
    return jnp.maximum(v, F32(0.0)) - (m * u) * (p * e)


PIECES = 3
LINE = HALO * PIECES


def pack_kernel(owners, feat_hbm, donor_hbm, accept_hbm, count, *refs):
    outs = refs[:owners]
    ends, donor, accept, sides, sem = refs[owners:]
    rows, channels = feat_hbm.shape
    piece = channels // PIECES
    loads = [
        pltpu.make_async_copy(feat_hbm.at[pl.ds(0, 8)], ends.at[0], sem.at[0]),
        pltpu.make_async_copy(feat_hbm.at[pl.ds(rows - 8, 8)], ends.at[1], sem.at[1]),
        pltpu.make_async_copy(donor_hbm, donor, sem.at[2]),
        pltpu.make_async_copy(accept_hbm, accept, sem.at[3]),
    ]
    for load in loads:
        load.start()
    for load in loads:
        load.wait()
    wanted = jnp.concatenate([donor[...], accept[...]], axis=1)
    width = wanted.shape[1]
    live = jnp.full((1, width), count[0], jnp.int32)
    line = jnp.concatenate([wanted >> 8, wanted & 255, live], axis=1).astype(F32)
    line = jnp.concatenate([line, jnp.zeros((1, piece - 3 * width), F32)], axis=1)
    for side, top in ((0, 0), (1, 8 - HALO)):
        end = ends[side].astype(F32)
        for h in range(HALO):
            for c in range(PIECES):
                place = h * PIECES + c
                sides[side, place : place + 1, :] = end[top + h : top + h + 1, c * piece : (c + 1) * piece]
        sides[side, LINE : LINE + 1, :] = line
        sides[side, LINE + 1 : 8, :] = jnp.zeros((8 - LINE - 1, piece), F32)
    first = sides[0]
    last = sides[1]
    me = lax.axis_index("seq")
    for k in range(owners):
        outs[k][...] = jnp.where((me ^ k) == me + 1, last, first).astype(BF16)


def pack(features, donor, accept, count, owners):
    rows, channels = features.shape
    slots = donor.shape[0]
    piece = channels // PIECES
    return pl.pallas_call(
        functools.partial(pack_kernel, owners),
        in_specs=[in_hbm()] * 3 + [pl.BlockSpec(memory_space=pltpu.SMEM)],
        out_specs=[whole()] * owners,
        out_shape=[vmem((8, piece), BF16)] * owners,
        scratch_shapes=[
            pltpu.VMEM((2, 8, channels), BF16),
            pltpu.VMEM((1, slots), jnp.int32),
            pltpu.VMEM((1, slots), jnp.int32),
            pltpu.VMEM((2, 8, piece), F32),
            pltpu.SemaphoreType.DMA((4,)),
        ],
        compiler_params=params(4),
        cost_estimate=pl.CostEstimate(flops=20000 * rows * channels, bytes_accessed=1 << 20, transcendentals=0),
        name="pack",
    )(far(features), far(donor.reshape(1, slots)), far(accept.reshape(1, slots)), count)


def unpack_line(packet_ref, width):
    line = packet_ref[...].astype(F32)[LINE : LINE + 1, 0 : 3 * width]
    wanted = line[:, 0:width] * F32(256.0) + line[:, width : 2 * width]
    lane = lax.broadcasted_iota(jnp.int32, (1, width), 1)
    slot = jnp.where(lane >= width // 2, lane - width // 2, lane).astype(F32)
    return wanted, slot < line[:, 2 * width :]


def strict_upper(size):
    a = lax.broadcasted_iota(jnp.int32, (size, size), 0)
    b = lax.broadcasted_iota(jnp.int32, (size, size), 1)
    return (a < b).astype(F32).astype(BF16)


def chosen(mine, capacity):
    ranks = jnp.dot(mine.astype(BF16), strict_upper(mine.shape[1]), preferred_element_type=F32)
    keyed = jnp.where(mine > F32(0.5), ranks, F32(-1.0))
    level = lax.broadcasted_iota(jnp.int32, (capacity, mine.shape[1]), 0).astype(F32)
    return lambda k: keyed[k : k + 1, :] == level


def conv_rows(load, taps_ref, gain_ref, columns, eps_scale):
    tap_count = taps_ref.shape[0]
    held = []
    total = None
    for j in range(columns):
        lanes = slice(j * LANES, (j + 1) * LANES)
        acc = None
        for k in range(tap_count):
            term = taps_ref[k : k + 1, lanes] * load(j, k)
            acc = term if acc is None else acc + term
        held.append(acc)
        total = acc * acc if total is None else total + acc * acc
    mean = jnp.sum(total, axis=-1, keepdims=True) * F32(eps_scale)
    scale = lax.rsqrt(mean + F32(1e-06))
    return [
        (held[j] * scale * gain_ref[0:1, j * LANES : (j + 1) * LANES]).astype(BF16)
        for j in range(columns)
    ]


def conv_kernel(
    owners,
    capacity,
    width,
    packet_ref,
    feat_ref,
    taps_ref,
    gain_ref,
    w_hbm,
    wd_ref,
    wa_ref,
    normed_ref,
    w_ref,
    spread_ref,
    wide,
    weight_sem,
):
    del wd_ref, wa_ref
    rows, channels = feat_ref.shape
    columns = channels // LANES
    parts = 4
    step = rows // parts
    weights = [pltpu.make_async_copy(w_hbm, w_ref, weight_sem.at[0])]
    for load in weights:
        load.start()

    me = lax.axis_index("seq")
    wanted, live = unpack_line(packet_ref, width)
    group = lax.broadcasted_iota(jnp.int32, (max(8, owners), width), 0)
    low = ((group ^ me) * rows).astype(F32)
    here = (wanted >= low) & (wanted < low + F32(rows)) & live & (group < owners)
    pick = chosen(jnp.where(here, F32(1.0), F32(0.0)), capacity)
    for k in range(owners):
        spread_ref[k * capacity : (k + 1) * capacity, :] = jnp.where(
            pick(k), F32(1.0), F32(0.0)
        ).astype(BF16)

    edge = jnp.zeros((8, LANES), F32)
    for j in range(columns):
        wide[j, 0:8, :] = edge
        wide[j, rows + 8 : rows + 16, :] = edge

    tile = 32

    def widen(c):
        for j in range(columns):
            lanes = slice(j * LANES, (j + 1) * LANES)
            wide[j, 8 + c * step : 8 + (c + 1) * step, :] = feat_ref[
                c * step : (c + 1) * step, lanes
            ].astype(F32)

    def convolve(first, count):
        def body(i, carry):
            base = pl.multiple_of(first + i * tile, tile)

            def load(j, k):
                return wide.at[j, pl.ds(base, tile + 16), :][8 - HALO + k : 8 - HALO + k + tile, :]

            out = conv_rows(load, taps_ref, gain_ref, columns, 1.0 / channels)
            for j in range(columns):
                normed_ref[pl.ds(base, tile), j * LANES : (j + 1) * LANES] = out[j]
            return carry

        lax.fori_loop(0, count, body, 0)

    widen(0)
    done = 0
    for c in range(1, parts):
        widen(c)
        ready = c * step // tile * tile
        convolve(done, (ready - done) // tile)
        done = ready
    convolve(done, (rows - done) // tile)
    for load in weights:
        load.wait()


def conv_norm(packet, features, taps, gain, w, wd, wa, owners, capacity, width):
    rows, channels = features.shape
    return pl.pallas_call(
        functools.partial(conv_kernel, owners, capacity, width),
        in_specs=[whole(), whole(), whole(), whole(), in_hbm(), whole(), whole()],
        out_specs=[whole()] * 3,
        out_shape=[
            vmem((rows, channels), BF16),
            vmem(w.shape, BF16),
            vmem((owners * capacity, width), BF16),
        ],
        scratch_shapes=[
            pltpu.VMEM((channels // LANES, rows + 16, LANES), F32),
            pltpu.SemaphoreType.DMA((1,)),
        ],
        compiler_params=params(6),
        cost_estimate=pl.CostEstimate(flops=20000 * rows * channels, bytes_accessed=12 << 20, transcendentals=rows),
        name="conv_norm",
    )(packet, features, taps, gain.reshape(1, channels), far(w), wd, wa)


def named_kernel(owners, capacity, width, *refs):
    packets = refs[:owners]
    feat_ref, normed_ref, taps_ref, gain_ref, w_ref, wd_ref, wa_ref = refs[owners : owners + 7]
    outs = refs[owners + 7 : 2 * owners + 7]
    patched_ref = refs[2 * owners + 7]
    near, lhs, res, enc, proj = refs[2 * owners + 8 :]
    del normed_ref
    rows, channels = feat_ref.shape
    columns = channels // LANES
    heads = wd_ref.shape[1]
    block = lhs.shape[0]
    me = lax.axis_index("seq")

    groups = max(8, owners)
    group = lax.broadcasted_iota(jnp.int32, (groups, width), 0)
    lane = lax.broadcasted_iota(jnp.int32, (1, width), 1)
    local = jnp.zeros((groups, width), F32)
    mine = jnp.zeros((groups, width), F32)
    start = (me * rows).astype(F32)
    for k in range(owners):
        at, live = unpack_line(packets[k], width)
        at = at - start
        here = (at >= F32(0.0)) & (at < F32(rows)) & live
        mine = jnp.where(group == k, jnp.where(here, F32(1.0), F32(0.0)), mine)
        local = jnp.where(group == k, at, local)
    ranks = jnp.dot(mine.astype(BF16), strict_upper(width), preferred_element_type=F32)
    sizes = jnp.sum(mine, axis=1, keepdims=True)
    total = jnp.sum(mine)
    blocks = (total.astype(jnp.int32) + (block - 1)) // block
    mark = F32(1 << 16)
    code = local + F32(1.0) + jnp.where(lane >= width // 2, mark, F32(0.0))
    offsets = []
    spots = []
    running = jnp.zeros((1, 1), F32)
    for k in range(owners):
        offsets.append(running)
        spots.append(jnp.where(mine[k : k + 1] > F32(0.5), ranks[k : k + 1] + running, F32(-1.0)))
        running = running + sizes[k : k + 1]

    piece = packets[0].shape[1]
    above = jnp.zeros((8, piece), F32)
    below = jnp.zeros((8, piece), F32)
    for k in range(1, owners):
        other = packets[k][...].astype(F32)
        above = jnp.where((me ^ k) == me - 1, other, above)
        below = jnp.where((me ^ k) == me + 1, other, below)
    span = 16
    foot_at = 16 + span
    after_at = foot_at + span + 8
    for j in range(columns):
        lanes = slice(j * LANES, (j + 1) * LANES)
        near[j, 8:foot_at, :] = feat_ref[0 : span + 8, lanes].astype(F32)
        near[j, foot_at:after_at, :] = feat_ref[rows - span - 8 : rows, lanes].astype(F32)
        part = j * LANES // piece
        inner = slice(j * LANES - part * piece, (j + 1) * LANES - part * piece)
        for h in range(HALO):
            row = h * PIECES + part
            near[j, 8 - HALO + h : 9 - HALO + h, :] = above[row : row + 1, inner]
            near[j, after_at + h : after_at + h + 1, :] = below[row : row + 1, inner]
    for origin, place in ((8, 0), (foot_at + 8, rows - span)):

        def load(j, k, origin=origin):
            begin = origin - HALO + k
            return near[j, begin : begin + span, :]

        out = conv_rows(load, taps_ref, gain_ref, columns, 1.0 / channels)
        for j in range(columns):
            patched_ref[place : place + span, j * LANES : (j + 1) * LANES] = out[j]

    for k in range(owners):
        outs[k][...] = jnp.zeros((capacity, heads), BF16)

    spread = lax.broadcasted_iota(jnp.int32, (block, rows), 1).astype(F32)
    level = lax.broadcasted_iota(jnp.int32, (block, width), 0).astype(F32)
    slot = lax.broadcasted_iota(jnp.int32, (capacity, block), 0).astype(F32)
    column = lax.broadcasted_iota(jnp.int32, (capacity, block), 1).astype(F32)
    wide = 256

    def body(c, carry):
        base = (c * block).astype(F32)
        found = jnp.zeros((block, width), F32)
        for k in range(owners):
            found = jnp.where(spots[k] - base == level, code[k : k + 1, :], found)
        found = jnp.sum(found, axis=1, keepdims=True)
        accepts = found >= mark
        index = found - jnp.where(accepts, mark, F32(0.0)) - F32(1.0)
        grab = jnp.where(spread == index, F32(1.0), F32(0.0)).astype(BF16)
        for j in range(channels // wide):
            lanes = slice(j * wide, (j + 1) * wide)
            lhs[:, lanes] = jnp.dot(grab, patched_ref[:, lanes], preferred_element_type=F32).astype(BF16)
            res[:, lanes] = jnp.dot(grab, feat_ref[:, lanes], preferred_element_type=F32).astype(BF16)
        for j in range(channels // wide):
            lanes = slice(j * wide, (j + 1) * wide)
            mixed = jnp.dot(lhs[...], w_ref[:, lanes], preferred_element_type=F32)
            enc[:, lanes] = (res[:, lanes].astype(F32) + gelu(mixed)).astype(BF16)
        for j in range(heads // wide):
            lanes = slice(j * wide, (j + 1) * wide)
            left = jnp.dot(enc[...], wd_ref[:, lanes], preferred_element_type=F32)
            right = jnp.dot(enc[...], wa_ref[:, lanes], preferred_element_type=F32)
            proj[:, lanes] = jnp.where(accepts, right, left).astype(BF16)
        for k in range(owners):
            put = (column + base == offsets[k] + slot) & (slot < sizes[k : k + 1])
            put = jnp.where(put, F32(1.0), F32(0.0)).astype(BF16)
            placed = jnp.dot(put, proj[...], preferred_element_type=F32)
            outs[k][...] = (outs[k][...].astype(F32) + placed).astype(BF16)
        return carry

    lax.fori_loop(0, blocks, body, 0)


def named(packets, feat, normed, taps, gain, w, wd, wa, width, capacity):
    owners = len(packets)
    rows, channels = feat.shape
    heads = wd.shape[1]
    block = 128
    out = pl.pallas_call(
        functools.partial(named_kernel, owners, capacity, width),
        in_specs=[whole()] * (owners + 7),
        out_specs=[whole()] * (owners + 1),
        out_shape=[vmem((capacity, heads), BF16)] * owners + [vmem((rows, channels), BF16)],
        input_output_aliases={owners + 1: owners},
        scratch_shapes=[
            pltpu.VMEM((channels // LANES, 72, LANES), F32),
            pltpu.VMEM((block, channels), BF16),
            pltpu.VMEM((block, channels), BF16),
            pltpu.VMEM((block, channels), BF16),
            pltpu.VMEM((block, heads), BF16),
        ],
        compiler_params=params(16),
        cost_estimate=pl.CostEstimate(
            flops=8 * block * channels * (channels + rows), bytes_accessed=8 << 20, transcendentals=2 * block * channels
        ),
        name="named_rows",
    )(*packets, feat, normed, taps, gain.reshape(1, channels), w, wd, wa)
    return out[:owners], out[owners]


def encode_kernel(normed_ref, feat_ref, w_ref, out_hbm, stage, sem):
    rows, channels = feat_ref.shape
    wide = 256
    tall = 512
    copies = []
    tall = rows // 2
    for i in range(2):
        part = slice(i * tall, (i + 1) * tall)
        for j in range(channels // wide):
            lanes = slice(j * wide, (j + 1) * wide)
            mixed = jnp.dot(normed_ref[part, :], w_ref[:, lanes], preferred_element_type=F32)
            stage[part, lanes] = (feat_ref[part, lanes].astype(F32) + gelu(mixed)).astype(BF16)
            if j % 2 == 1:
                at = pl.ds((j - 1) * wide, 2 * wide)
                copy = pltpu.make_async_copy(
                    stage.at[pl.ds(i * tall, tall), at], out_hbm.at[pl.ds(i * tall, tall), at], sem.at[i * 3 + j // 2]
                )
                copy.start()
                copies.append(copy)
    for copy in copies:
        copy.wait()


def encode(normed, feat, w):
    rows, channels = feat.shape
    return pl.pallas_call(
        encode_kernel,
        in_specs=[whole()] * 3,
        out_specs=pl.BlockSpec(memory_space=pltpu.MemorySpace.HBM),
        out_shape=jax.ShapeDtypeStruct((rows, channels), BF16),
        scratch_shapes=[pltpu.VMEM((rows, channels), BF16), pltpu.SemaphoreType.DMA((channels // 256,))],
        compiler_params=params(6),
        cost_estimate=pl.CostEstimate(
            flops=2 * rows * channels * channels, bytes_accessed=8 << 20, transcendentals=2 * rows * channels
        ),
        name="encode",
    )(normed, feat, w)


def junction_kernel(owners, *refs):
    blocks = refs[:owners]
    spread_ref, out_ref = refs[owners:]
    slots = out_ref.shape[0]
    capacity = blocks[0].shape[0]
    picked = None
    for k in range(owners):
        part = lax.dot_general(
            spread_ref[k * capacity : (k + 1) * capacity, :],
            blocks[k][...],
            (((0,), (0,)), ((), ())),
            preferred_element_type=F32,
        )
        picked = part if picked is None else picked + part
    left, right = picked[:slots], picked[slots:]
    silu = left / (F32(1.0) + jnp.exp(-left))
    out_ref[...] = (silu * right).astype(BF16)


def junction(blocks, spread):
    slots = spread.shape[1] // 2
    heads = blocks[0].shape[1]
    return pl.pallas_call(
        functools.partial(junction_kernel, len(blocks)),
        in_specs=[whole()] * (len(blocks) + 1),
        out_specs=whole(),
        out_shape=jax.ShapeDtypeStruct((slots, heads), BF16),
        compiler_params=params(6),
        name="junction",
    )(*blocks, spread)


def swap_all(arrays):
    owners = len(arrays)
    got = [arrays[0]]
    for k in range(1, owners):
        got.append(lax.ppermute(arrays[k], "seq", [(i, i ^ k) for i in range(owners)]))
    return got


def on_device(
    features,
    conv_taps,
    norm_gain,
    point_weight,
    donor_weight,
    accept_weight,
    donor_pos,
    accept_pos,
    pair_counts,
):
    slots = donor_pos.shape[0]
    owners = lax.axis_size("seq")
    capacity = 2 * ((2 * slots + owners - 1) // owners)
    own = pack(features, donor_pos, accept_pos, pair_counts, owners)
    packets = swap_all(own)
    width = 2 * slots
    normed, w, spread = conv_norm(
        own[0], features, conv_taps, norm_gain, point_weight, donor_weight, accept_weight, owners, capacity, width
    )
    sends, patched = named(
        packets, features, normed, conv_taps, norm_gain, w, donor_weight, accept_weight, width, capacity
    )
    blocks = swap_all(sends)
    encoded = encode(patched, features, w)
    return encoded, junction(blocks, spread)


def solution(mesh):
    placed = (
        P(("dp", "seq"), None),
        P(),
        P(),
        P(),
        P(),
        P(),
        P(("dp", "seq")),
        P(("dp", "seq")),
        P(("dp", "seq")),
    )

    return jax.shard_map(
        on_device,
        mesh=mesh,
        in_specs=placed,
        out_specs=(P(("dp", "seq"), None), P(("dp", "seq"), None)),
        check_vma=False,
    )
```

```python
import functools

import jax
import jax.numpy as jnp
from jax import lax
from jax.experimental import pallas as pl
from jax.experimental.pallas import tpu as pltpu
from jax.sharding import PartitionSpec as P


F32 = jnp.float32
BF16 = jnp.bfloat16
LANES = 128
HALO = 2
MIB = 1 << 20


def vmem(shape, dtype):
    return pltpu.VMEM(shape, dtype)


def whole():
    return pl.BlockSpec(memory_space=pltpu.VMEM)


def far(array):
    return pltpu.with_memory_space_constraint(array, pltpu.MemorySpace.HBM)


def in_hbm():
    return pl.BlockSpec(memory_space=pltpu.MemorySpace.HBM)


def params(mib):
    return pltpu.CompilerParams(vmem_limit_bytes=mib * MIB)


def gelu(v):
    m = jnp.abs(v)
    d = m * F32(0.3275911 * 0.7071067811865476) + F32(1.0)
    u = pl.reciprocal(d, approx=False)
    p = u * F32(0.5 * 1.061405429) + F32(0.5 * -1.453152027)
    p = p * u + F32(0.5 * 1.421413741)
    p = p * u + F32(0.5 * -0.284496736)
    p = p * u + F32(0.5 * 0.254829592)
    e = jnp.exp2(v * v * F32(-0.5 * 1.4426950408889634))
    return jnp.maximum(v, F32(0.0)) - (m * u) * (p * e)


PIECES = 3
LINE = HALO * PIECES


def pack_kernel(owners, feat_hbm, donor_hbm, accept_hbm, count, *refs):
    outs = refs[:owners]
    ends, donor, accept, sides, sem = refs[owners:]
    rows, channels = feat_hbm.shape
    piece = channels // PIECES
    loads = [
        pltpu.make_async_copy(feat_hbm.at[pl.ds(0, 8)], ends.at[0], sem.at[0]),
        pltpu.make_async_copy(feat_hbm.at[pl.ds(rows - 8, 8)], ends.at[1], sem.at[1]),
        pltpu.make_async_copy(donor_hbm, donor, sem.at[2]),
        pltpu.make_async_copy(accept_hbm, accept, sem.at[3]),
    ]
    for load in loads:
        load.start()
    for load in loads:
        load.wait()
    wanted = jnp.concatenate([donor[...], accept[...]], axis=1)
    width = wanted.shape[1]
    live = jnp.full((1, width), count[0], jnp.int32)
    line = jnp.concatenate([wanted >> 8, wanted & 255, live], axis=1).astype(F32)
    line = jnp.concatenate([line, jnp.zeros((1, piece - 3 * width), F32)], axis=1)
    for side, top in ((0, 0), (1, 8 - HALO)):
        end = ends[side].astype(F32)
        for h in range(HALO):
            for c in range(PIECES):
                place = h * PIECES + c
                sides[side, place : place + 1, :] = end[top + h : top + h + 1, c * piece : (c + 1) * piece]
        sides[side, LINE : LINE + 1, :] = line
        sides[side, LINE + 1 : 8, :] = jnp.zeros((8 - LINE - 1, piece), F32)
    first = sides[0]
    last = sides[1]
    me = lax.axis_index("seq")
    for k in range(owners):
        outs[k][...] = jnp.where((me ^ k) == me + 1, last, first).astype(BF16)


def pack(features, donor, accept, count, owners):
    rows, channels = features.shape
    slots = donor.shape[0]
    piece = channels // PIECES
    return pl.pallas_call(
        functools.partial(pack_kernel, owners),
        in_specs=[in_hbm()] * 3 + [pl.BlockSpec(memory_space=pltpu.SMEM)],
        out_specs=[whole()] * owners,
        out_shape=[vmem((8, piece), BF16)] * owners,
        scratch_shapes=[
            pltpu.VMEM((2, 8, channels), BF16),
            pltpu.VMEM((1, slots), jnp.int32),
            pltpu.VMEM((1, slots), jnp.int32),
            pltpu.VMEM((2, 8, piece), F32),
            pltpu.SemaphoreType.DMA((4,)),
        ],
        compiler_params=params(4),
        cost_estimate=pl.CostEstimate(flops=20000 * rows * channels, bytes_accessed=1 << 20, transcendentals=0),
        name="pack",
    )(far(features), far(donor.reshape(1, slots)), far(accept.reshape(1, slots)), count)


def unpack_line(packet_ref, width):
    line = packet_ref[...].astype(F32)[LINE : LINE + 1, 0 : 3 * width]
    wanted = line[:, 0:width] * F32(256.0) + line[:, width : 2 * width]
    lane = lax.broadcasted_iota(jnp.int32, (1, width), 1)
    slot = jnp.where(lane >= width // 2, lane - width // 2, lane).astype(F32)
    return wanted, slot < line[:, 2 * width :]


def strict_upper(size):
    a = lax.broadcasted_iota(jnp.int32, (size, size), 0)
    b = lax.broadcasted_iota(jnp.int32, (size, size), 1)
    return (a < b).astype(F32).astype(BF16)


def chosen(mine, capacity):
    ranks = jnp.dot(mine.astype(BF16), strict_upper(mine.shape[1]), preferred_element_type=F32)
    keyed = jnp.where(mine > F32(0.5), ranks, F32(-1.0))
    level = lax.broadcasted_iota(jnp.int32, (capacity, mine.shape[1]), 0).astype(F32)
    return lambda k: keyed[k : k + 1, :] == level


def conv_rows(load, taps_ref, gain_ref, columns, eps_scale):
    tap_count = taps_ref.shape[0]
    held = []
    total = None
    for j in range(columns):
        lanes = slice(j * LANES, (j + 1) * LANES)
        acc = None
        for k in range(tap_count):
            term = taps_ref[k : k + 1, lanes] * load(j, k)
            acc = term if acc is None else acc + term
        held.append(acc)
        total = acc * acc if total is None else total + acc * acc
    mean = jnp.sum(total, axis=-1, keepdims=True) * F32(eps_scale)
    scale = lax.rsqrt(mean + F32(1e-06))
    return [
        (held[j] * scale * gain_ref[0:1, j * LANES : (j + 1) * LANES]).astype(BF16)
        for j in range(columns)
    ]


def conv_kernel(
    owners,
    capacity,
    width,
    packet_ref,
    feat_ref,
    taps_ref,
    gain_ref,
    w_ref,
    wd_ref,
    wa_hbm,
    normed_ref,
    wa_ref,
    spread_ref,
    wide,
    mixed,
    squares,
    weight_sem,
):
    del w_ref, wd_ref
    rows, channels = feat_ref.shape
    columns = channels // LANES
    weights = [pltpu.make_async_copy(wa_hbm, wa_ref, weight_sem.at[0])]
    for load in weights:
        load.start()

    me = lax.axis_index("seq")
    wanted, live = unpack_line(packet_ref, width)
    group = lax.broadcasted_iota(jnp.int32, (max(8, owners), width), 0)
    low = ((group ^ me) * rows).astype(F32)
    here = (wanted >= low) & (wanted < low + F32(rows)) & live & (group < owners)
    pick = chosen(jnp.where(here, F32(1.0), F32(0.0)), capacity)
    for k in range(owners):
        spread_ref[k * capacity : (k + 1) * capacity, :] = jnp.where(
            pick(k), F32(1.0), F32(0.0)
        ).astype(BF16)

    edge = jnp.zeros((8, LANES), F32)
    for j in range(columns):
        wide[j, 0:8, :] = edge
        wide[j, rows + 8 : rows + 16, :] = edge

    tile = 32
    tap_count = taps_ref.shape[0]

    for j in range(columns):
        lanes = slice(j * LANES, (j + 1) * LANES)
        wide[j, 8 : 8 + rows, :] = feat_ref[:, lanes].astype(F32)

    def convolve(i, carry):
        base = pl.multiple_of(i * tile, tile)
        total = None
        for j in range(columns):
            lanes = slice(j * LANES, (j + 1) * LANES)
            acc = None
            for k in range(tap_count):
                begin = 8 - HALO + k
                part = wide.at[j, pl.ds(base, tile + 16), :][begin : begin + tile, :]
                term = taps_ref[k : k + 1, lanes] * part
                acc = term if acc is None else acc + term
            mixed[j, pl.ds(base, tile), :] = acc
            total = acc * acc if total is None else total + acc * acc
        squares[pl.ds(base, tile), :] = total
        return carry

    lax.fori_loop(0, rows // tile, convolve, 0, unroll=2)
    mean = jnp.sum(squares[...], axis=-1, keepdims=True) * F32(1.0 / channels)
    squares[...] = jnp.broadcast_to(lax.rsqrt(mean + F32(1e-06)), (rows, LANES))

    def scale(i, carry):
        base = pl.multiple_of(i * tile, tile)
        by = squares[pl.ds(base, tile), :]
        for j in range(columns):
            lanes = slice(j * LANES, (j + 1) * LANES)
            out = mixed[j, pl.ds(base, tile), :] * by * gain_ref[0:1, lanes]
            normed_ref[pl.ds(base, tile), lanes] = out.astype(BF16)
        return carry

    lax.fori_loop(0, rows // tile, scale, 0)
    for load in weights:
        load.wait()


def conv_norm(packet, features, taps, gain, w, wd, wa, owners, capacity, width):
    rows, channels = features.shape
    return pl.pallas_call(
        functools.partial(conv_kernel, owners, capacity, width),
        in_specs=[whole(), whole(), whole(), whole(), whole(), whole(), in_hbm()],
        out_specs=[whole()] * 3,
        out_shape=[
            vmem((rows, channels), BF16),
            vmem(wa.shape, BF16),
            vmem((owners * capacity, width), BF16),
        ],
        scratch_shapes=[
            pltpu.VMEM((channels // LANES, rows + 16, LANES), F32),
            pltpu.VMEM((channels // LANES, rows, LANES), F32),
            pltpu.VMEM((rows, LANES), F32),
            pltpu.SemaphoreType.DMA((1,)),
        ],
        compiler_params=params(10),
        cost_estimate=pl.CostEstimate(flops=20000 * rows * channels, bytes_accessed=12 << 20, transcendentals=rows),
        name="conv_norm",
    )(packet, features, taps, gain.reshape(1, channels), w, wd, far(wa))


def named_kernel(owners, capacity, width, *refs):
    packets = refs[:owners]
    feat_ref, normed_ref, taps_ref, gain_ref, w_ref, wd_ref, wa_ref = refs[owners : owners + 7]
    outs = refs[owners + 7 : 2 * owners + 7]
    patched_ref = refs[2 * owners + 7]
    near, lhs, res, enc, proj = refs[2 * owners + 8 :]
    del normed_ref
    rows, channels = feat_ref.shape
    columns = channels // LANES
    heads = wd_ref.shape[1]
    block = lhs.shape[0]
    me = lax.axis_index("seq")

    groups = max(8, owners)
    group = lax.broadcasted_iota(jnp.int32, (groups, width), 0)
    lane = lax.broadcasted_iota(jnp.int32, (1, width), 1)
    local = jnp.zeros((groups, width), F32)
    mine = jnp.zeros((groups, width), F32)
    start = (me * rows).astype(F32)
    for k in range(owners):
        at, live = unpack_line(packets[k], width)
        at = at - start
        here = (at >= F32(0.0)) & (at < F32(rows)) & live
        mine = jnp.where(group == k, jnp.where(here, F32(1.0), F32(0.0)), mine)
        local = jnp.where(group == k, at, local)
    ranks = jnp.dot(mine.astype(BF16), strict_upper(width), preferred_element_type=F32)
    sizes = jnp.sum(mine, axis=1, keepdims=True)
    total = jnp.sum(mine)
    blocks = (total.astype(jnp.int32) + (block - 1)) // block
    mark = F32(1 << 16)
    code = local + F32(1.0) + jnp.where(lane >= width // 2, mark, F32(0.0))
    offsets = []
    spots = []
    running = jnp.zeros((1, 1), F32)
    for k in range(owners):
        offsets.append(running)
        spots.append(jnp.where(mine[k : k + 1] > F32(0.5), ranks[k : k + 1] + running, F32(-1.0)))
        running = running + sizes[k : k + 1]

    piece = packets[0].shape[1]
    above = jnp.zeros((8, piece), F32)
    below = jnp.zeros((8, piece), F32)
    for k in range(1, owners):
        other = packets[k][...].astype(F32)
        above = jnp.where((me ^ k) == me - 1, other, above)
        below = jnp.where((me ^ k) == me + 1, other, below)
    span = 16
    foot_at = 16 + span
    after_at = foot_at + span + 8
    for j in range(columns):
        lanes = slice(j * LANES, (j + 1) * LANES)
        near[j, 8:foot_at, :] = feat_ref[0 : span + 8, lanes].astype(F32)
        near[j, foot_at:after_at, :] = feat_ref[rows - span - 8 : rows, lanes].astype(F32)
        part = j * LANES // piece
        inner = slice(j * LANES - part * piece, (j + 1) * LANES - part * piece)
        for h in range(HALO):
            row = h * PIECES + part
            near[j, 8 - HALO + h : 9 - HALO + h, :] = above[row : row + 1, inner]
            near[j, after_at + h : after_at + h + 1, :] = below[row : row + 1, inner]
    for origin, place in ((8, 0), (foot_at + 8, rows - span)):

        def load(j, k, origin=origin):
            begin = origin - HALO + k
            return near[j, begin : begin + span, :]

        out = conv_rows(load, taps_ref, gain_ref, columns, 1.0 / channels)
        for j in range(columns):
            patched_ref[place : place + span, j * LANES : (j + 1) * LANES] = out[j]

    spread = lax.broadcasted_iota(jnp.int32, (block, rows), 1).astype(F32)
    level = lax.broadcasted_iota(jnp.int32, (block, width), 0).astype(F32)
    slot = lax.broadcasted_iota(jnp.int32, (capacity, block), 0).astype(F32)
    column = lax.broadcasted_iota(jnp.int32, (capacity, block), 1).astype(F32)
    wide = 256

    def encode_block(c, store):
        base = F32(c * block) if isinstance(c, int) else (c * block).astype(F32)
        found = jnp.zeros((block, width), F32)
        for k in range(owners):
            found = jnp.where(spots[k] - base == level, code[k : k + 1, :], found)
        found = jnp.sum(found, axis=1, keepdims=True)
        accepts = found >= mark
        index = found - jnp.where(accepts, mark, F32(0.0)) - F32(1.0)
        grab = jnp.where(spread == index, F32(1.0), F32(0.0)).astype(BF16)
        for j in range(channels // wide):
            lanes = slice(j * wide, (j + 1) * wide)
            lhs[:, lanes] = jnp.dot(grab, patched_ref[:, lanes], preferred_element_type=F32).astype(BF16)
            res[:, lanes] = jnp.dot(grab, feat_ref[:, lanes], preferred_element_type=F32).astype(BF16)
        for j in range(channels // wide):
            lanes = slice(j * wide, (j + 1) * wide)
            mixed = jnp.dot(lhs[...], w_ref[:, lanes], preferred_element_type=F32)
            enc[:, lanes] = (res[:, lanes].astype(F32) + gelu(mixed)).astype(BF16)
        for j in range(heads // wide):
            lanes = slice(j * wide, (j + 1) * wide)
            left = jnp.dot(enc[...], wd_ref[:, lanes], preferred_element_type=F32)
            right = jnp.dot(enc[...], wa_ref[:, lanes], preferred_element_type=F32)
            proj[:, lanes] = jnp.where(accepts, right, left).astype(BF16)
        for k in range(owners):
            put = (column + base == offsets[k] + slot) & (slot < sizes[k : k + 1])
            put = jnp.where(put, F32(1.0), F32(0.0)).astype(BF16)
            placed = jnp.dot(put, proj[...], preferred_element_type=F32)
            store(outs[k], placed)

    def write(ref, value):
        ref[...] = value.astype(BF16)

    def add(ref, value):
        ref[...] = (ref[...].astype(F32) + value).astype(BF16)

    encode_block(0, write)

    def body(c, carry):
        encode_block(c, add)
        return carry

    lax.fori_loop(1, blocks, body, 0)


def named(packets, feat, normed, taps, gain, w, wd, wa, width, capacity):
    owners = len(packets)
    rows, channels = feat.shape
    heads = wd.shape[1]
    block = 128
    out = pl.pallas_call(
        functools.partial(named_kernel, owners, capacity, width),
        in_specs=[whole()] * (owners + 7),
        out_specs=[whole()] * (owners + 1),
        out_shape=[vmem((capacity, heads), BF16)] * owners + [vmem((rows, channels), BF16)],
        input_output_aliases={owners + 1: owners},
        scratch_shapes=[
            pltpu.VMEM((channels // LANES, 72, LANES), F32),
            pltpu.VMEM((block, channels), BF16),
            pltpu.VMEM((block, channels), BF16),
            pltpu.VMEM((block, channels), BF16),
            pltpu.VMEM((block, heads), BF16),
        ],
        compiler_params=params(16),
        cost_estimate=pl.CostEstimate(
            flops=8 * block * channels * (channels + rows), bytes_accessed=8 << 20, transcendentals=2 * block * channels
        ),
        name="named_rows",
    )(*packets, feat, normed, taps, gain.reshape(1, channels), w, wd, wa)
    return out[:owners], out[owners]


def encode_kernel(normed_ref, feat_ref, w_ref, out_hbm, stage, sem):
    rows, channels = feat_ref.shape
    wide = 256
    tall = 512
    copies = []
    tall = rows // 2
    for i in range(2):
        part = slice(i * tall, (i + 1) * tall)
        for j in range(channels // wide):
            lanes = slice(j * wide, (j + 1) * wide)
            mixed = jnp.dot(normed_ref[part, :], w_ref[:, lanes], preferred_element_type=F32)
            stage[part, lanes] = (feat_ref[part, lanes].astype(F32) + gelu(mixed)).astype(BF16)
            if j % 2 == 1:
                at = pl.ds((j - 1) * wide, 2 * wide)
                copy = pltpu.make_async_copy(
                    stage.at[pl.ds(i * tall, tall), at], out_hbm.at[pl.ds(i * tall, tall), at], sem.at[i * 3 + j // 2]
                )
                copy.start()
                copies.append(copy)
    for copy in copies:
        copy.wait()


def encode(normed, feat, w):
    rows, channels = feat.shape
    return pl.pallas_call(
        encode_kernel,
        in_specs=[whole()] * 3,
        out_specs=pl.BlockSpec(memory_space=pltpu.MemorySpace.HBM),
        out_shape=jax.ShapeDtypeStruct((rows, channels), BF16),
        scratch_shapes=[pltpu.VMEM((rows, channels), BF16), pltpu.SemaphoreType.DMA((channels // 256,))],
        compiler_params=params(6),
        cost_estimate=pl.CostEstimate(
            flops=2 * rows * channels * channels, bytes_accessed=8 << 20, transcendentals=2 * rows * channels
        ),
        name="encode",
    )(normed, feat, w)


def junction_kernel(owners, *refs):
    blocks = refs[:owners]
    spread_ref, out_ref = refs[owners:]
    slots = out_ref.shape[0]
    capacity = blocks[0].shape[0]
    picked = None
    for k in range(owners):
        part = lax.dot_general(
            spread_ref[k * capacity : (k + 1) * capacity, :],
            blocks[k][...],
            (((0,), (0,)), ((), ())),
            preferred_element_type=F32,
        )
        picked = part if picked is None else picked + part
    left, right = picked[:slots], picked[slots:]
    silu = left / (F32(1.0) + jnp.exp(-left))
    out_ref[...] = (silu * right).astype(BF16)


def junction(blocks, spread):
    slots = spread.shape[1] // 2
    heads = blocks[0].shape[1]
    return pl.pallas_call(
        functools.partial(junction_kernel, len(blocks)),
        in_specs=[whole()] * (len(blocks) + 1),
        out_specs=whole(),
        out_shape=jax.ShapeDtypeStruct((slots, heads), BF16),
        compiler_params=params(6),
        name="junction",
    )(*blocks, spread)


def swap_all(arrays):
    owners = len(arrays)
    got = [arrays[0]]
    for k in range(1, owners):
        got.append(lax.ppermute(arrays[k], "seq", [(i, i ^ k) for i in range(owners)]))
    return got


def on_device(
    features,
    conv_taps,
    norm_gain,
    point_weight,
    donor_weight,
    accept_weight,
    donor_pos,
    accept_pos,
    pair_counts,
):
    slots = donor_pos.shape[0]
    owners = lax.axis_size("seq")
    capacity = 2 * ((2 * slots + owners - 1) // owners)
    own = pack(features, donor_pos, accept_pos, pair_counts, owners)
    packets = swap_all(own)
    width = 2 * slots
    normed, wa, spread = conv_norm(
        own[0], features, conv_taps, norm_gain, point_weight, donor_weight, accept_weight, owners, capacity, width
    )
    sends, patched = named(
        packets, features, normed, conv_taps, norm_gain, point_weight, donor_weight, wa, width, capacity
    )
    blocks = swap_all(sends)
    encoded = encode(patched, features, point_weight)
    return encoded, junction(blocks, spread)


def solution(mesh):
    placed = (
        P(("dp", "seq"), None),
        P(),
        P(),
        P(),
        P(),
        P(),
        P(("dp", "seq")),
        P(("dp", "seq")),
        P(("dp", "seq")),
    )

    return jax.shard_map(
        on_device,
        mesh=mesh,
        in_specs=placed,
        out_specs=(P(("dp", "seq"), None), P(("dp", "seq"), None)),
        check_vma=False,
    )
```

```python
import functools

import jax
import jax.numpy as jnp
from jax import lax
from jax.experimental import pallas as pl
from jax.experimental.pallas import tpu as pltpu
from jax.sharding import PartitionSpec as P


F32 = jnp.float32
BF16 = jnp.bfloat16
LANES = 128
HALO = 2
MIB = 1 << 20


def vmem(shape, dtype):
    return pltpu.VMEM(shape, dtype)


def whole():
    return pl.BlockSpec(memory_space=pltpu.VMEM)


def far(array):
    return pltpu.with_memory_space_constraint(array, pltpu.MemorySpace.HBM)


def in_hbm():
    return pl.BlockSpec(memory_space=pltpu.MemorySpace.HBM)


def params(mib):
    return pltpu.CompilerParams(vmem_limit_bytes=mib * MIB)


def gelu(v):
    m = jnp.abs(v)
    d = m * F32(0.3275911 * 0.7071067811865476) + F32(1.0)
    u = pl.reciprocal(d, approx=False)
    p = u * F32(0.5 * 1.061405429) + F32(0.5 * -1.453152027)
    p = p * u + F32(0.5 * 1.421413741)
    p = p * u + F32(0.5 * -0.284496736)
    p = p * u + F32(0.5 * 0.254829592)
    e = jnp.exp2(v * v * F32(-0.5 * 1.4426950408889634))
    return jnp.maximum(v, F32(0.0)) - (m * u) * (p * e)


PIECES = 3
LINE = HALO * PIECES


def pack_kernel(owners, feat_hbm, donor_hbm, accept_hbm, count, *refs):
    outs = refs[:owners]
    ends, donor, accept, sides, sem = refs[owners:]
    rows, channels = feat_hbm.shape
    piece = channels // PIECES
    loads = [
        pltpu.make_async_copy(feat_hbm.at[pl.ds(0, 8)], ends.at[0], sem.at[0]),
        pltpu.make_async_copy(feat_hbm.at[pl.ds(rows - 8, 8)], ends.at[1], sem.at[1]),
        pltpu.make_async_copy(donor_hbm, donor, sem.at[2]),
        pltpu.make_async_copy(accept_hbm, accept, sem.at[3]),
    ]
    for load in loads:
        load.start()
    for load in loads:
        load.wait()
    wanted = jnp.concatenate([donor[...], accept[...]], axis=1)
    width = wanted.shape[1]
    live = jnp.full((1, width), count[0], jnp.int32)
    line = jnp.concatenate([wanted >> 8, wanted & 255, live], axis=1).astype(F32)
    line = jnp.concatenate([line, jnp.zeros((1, piece - 3 * width), F32)], axis=1)
    for side, top in ((0, 0), (1, 8 - HALO)):
        end = ends[side].astype(F32)
        for h in range(HALO):
            for c in range(PIECES):
                place = h * PIECES + c
                sides[side, place : place + 1, :] = end[top + h : top + h + 1, c * piece : (c + 1) * piece]
        sides[side, LINE : LINE + 1, :] = line
        sides[side, LINE + 1 : 8, :] = jnp.zeros((8 - LINE - 1, piece), F32)
    first = sides[0]
    last = sides[1]
    me = lax.axis_index("seq")
    for k in range(owners):
        outs[k][...] = jnp.where((me ^ k) == me + 1, last, first).astype(BF16)


def pack(features, donor, accept, count, owners):
    rows, channels = features.shape
    slots = donor.shape[0]
    piece = channels // PIECES
    return pl.pallas_call(
        functools.partial(pack_kernel, owners),
        in_specs=[in_hbm()] * 3 + [pl.BlockSpec(memory_space=pltpu.SMEM)],
        out_specs=[whole()] * owners,
        out_shape=[vmem((8, piece), BF16)] * owners,
        scratch_shapes=[
            pltpu.VMEM((2, 8, channels), BF16),
            pltpu.VMEM((1, slots), jnp.int32),
            pltpu.VMEM((1, slots), jnp.int32),
            pltpu.VMEM((2, 8, piece), F32),
            pltpu.SemaphoreType.DMA((4,)),
        ],
        compiler_params=params(4),
        cost_estimate=pl.CostEstimate(flops=20000 * rows * channels, bytes_accessed=1 << 20, transcendentals=0),
        name="pack",
    )(far(features), far(donor.reshape(1, slots)), far(accept.reshape(1, slots)), count)


def unpack_line(packet_ref, width):
    line = packet_ref[...].astype(F32)[LINE : LINE + 1, 0 : 3 * width]
    wanted = line[:, 0:width] * F32(256.0) + line[:, width : 2 * width]
    lane = lax.broadcasted_iota(jnp.int32, (1, width), 1)
    slot = jnp.where(lane >= width // 2, lane - width // 2, lane).astype(F32)
    return wanted, slot < line[:, 2 * width :]


def strict_upper(size):
    a = lax.broadcasted_iota(jnp.int32, (size, size), 0)
    b = lax.broadcasted_iota(jnp.int32, (size, size), 1)
    return (a < b).astype(F32).astype(BF16)


def chosen(mine, capacity):
    ranks = jnp.dot(mine.astype(BF16), strict_upper(mine.shape[1]), preferred_element_type=F32)
    keyed = jnp.where(mine > F32(0.5), ranks, F32(-1.0))
    level = lax.broadcasted_iota(jnp.int32, (capacity, mine.shape[1]), 0).astype(F32)
    return lambda k: keyed[k : k + 1, :] == level


def conv_rows(load, taps_ref, gain_ref, columns, eps_scale):
    tap_count = taps_ref.shape[0]
    held = []
    total = None
    for j in range(columns):
        lanes = slice(j * LANES, (j + 1) * LANES)
        acc = None
        for k in range(tap_count):
            term = taps_ref[k : k + 1, lanes] * load(j, k)
            acc = term if acc is None else acc + term
        held.append(acc)
        total = acc * acc if total is None else total + acc * acc
    mean = jnp.sum(total, axis=-1, keepdims=True) * F32(eps_scale)
    scale = lax.rsqrt(mean + F32(1e-06))
    return [
        (held[j] * scale * gain_ref[0:1, j * LANES : (j + 1) * LANES]).astype(BF16)
        for j in range(columns)
    ]


def conv_kernel(
    owners,
    capacity,
    width,
    packet_ref,
    feat_ref,
    taps_ref,
    gain_ref,
    w_ref,
    wd_ref,
    wa_hbm,
    normed_ref,
    wa_ref,
    spread_ref,
    wide,
    mixed,
    squares,
    weight_sem,
):
    del w_ref, wd_ref
    rows, channels = feat_ref.shape
    columns = channels // LANES
    weights = [pltpu.make_async_copy(wa_hbm, wa_ref, weight_sem.at[0])]
    for load in weights:
        load.start()

    me = lax.axis_index("seq")
    wanted, live = unpack_line(packet_ref, width)
    group = lax.broadcasted_iota(jnp.int32, (max(8, owners), width), 0)
    low = ((group ^ me) * rows).astype(F32)
    here = (wanted >= low) & (wanted < low + F32(rows)) & live & (group < owners)
    pick = chosen(jnp.where(here, F32(1.0), F32(0.0)), capacity)
    for k in range(owners):
        spread_ref[k * capacity : (k + 1) * capacity, :] = jnp.where(
            pick(k), F32(1.0), F32(0.0)
        ).astype(BF16)

    edge = jnp.zeros((8, LANES), F32)
    for j in range(columns):
        wide[j, 0:8, :] = edge
        wide[j, rows + 8 : rows + 16, :] = edge

    tile = 32
    tap_count = taps_ref.shape[0]

    for j in range(columns):
        lanes = slice(j * LANES, (j + 1) * LANES)
        wide[j, 8 : 8 + rows, :] = feat_ref[:, lanes].astype(F32)

    def convolve(i, carry):
        base = pl.multiple_of(i * tile, tile)
        total = None
        for j in range(columns):
            lanes = slice(j * LANES, (j + 1) * LANES)
            acc = None
            for k in range(tap_count):
                begin = 8 - HALO + k
                part = wide.at[j, pl.ds(base, tile + 16), :][begin : begin + tile, :]
                term = taps_ref[k : k + 1, lanes] * part
                acc = term if acc is None else acc + term
            mixed[j, pl.ds(base, tile), :] = acc
            total = acc * acc if total is None else total + acc * acc
        squares[pl.ds(base, tile), :] = total
        return carry

    lax.fori_loop(0, rows // tile, convolve, 0, unroll=2)
    mean = jnp.sum(squares[...], axis=-1, keepdims=True) * F32(1.0 / channels)
    squares[...] = jnp.broadcast_to(lax.rsqrt(mean + F32(1e-06)), (rows, LANES))

    def scale(i, carry):
        base = pl.multiple_of(i * tile, tile)
        by = squares[pl.ds(base, tile), :]
        for j in range(columns):
            lanes = slice(j * LANES, (j + 1) * LANES)
            out = mixed[j, pl.ds(base, tile), :] * by * gain_ref[0:1, lanes]
            normed_ref[pl.ds(base, tile), lanes] = out.astype(BF16)
        return carry

    lax.fori_loop(0, rows // tile, scale, 0)
    for load in weights:
        load.wait()


def conv_norm(packet, features, taps, gain, w, wd, wa, owners, capacity, width):
    rows, channels = features.shape
    return pl.pallas_call(
        functools.partial(conv_kernel, owners, capacity, width),
        in_specs=[whole(), whole(), whole(), whole(), whole(), whole(), in_hbm()],
        out_specs=[whole()] * 3,
        out_shape=[
            vmem((rows, channels), BF16),
            vmem(wa.shape, BF16),
            vmem((owners * capacity, width), BF16),
        ],
        scratch_shapes=[
            pltpu.VMEM((channels // LANES, rows + 16, LANES), F32),
            pltpu.VMEM((channels // LANES, rows, LANES), F32),
            pltpu.VMEM((rows, LANES), F32),
            pltpu.SemaphoreType.DMA((1,)),
        ],
        compiler_params=params(10),
        cost_estimate=pl.CostEstimate(flops=20000 * rows * channels, bytes_accessed=12 << 20, transcendentals=rows),
        name="conv_norm",
    )(packet, features, taps, gain.reshape(1, channels), w, wd, far(wa))


def named_kernel(owners, capacity, width, *refs):
    packets = refs[:owners]
    feat_ref, normed_ref, taps_ref, gain_ref, w_ref, wd_ref, wa_ref = refs[owners : owners + 7]
    outs = refs[owners + 7 : 2 * owners + 7]
    patched_ref = refs[2 * owners + 7]
    near, lhs, res, enc, proj = refs[2 * owners + 8 :]
    del normed_ref
    rows, channels = feat_ref.shape
    columns = channels // LANES
    heads = wd_ref.shape[1]
    block = lhs.shape[0]
    me = lax.axis_index("seq")

    groups = max(8, owners)
    group = lax.broadcasted_iota(jnp.int32, (groups, width), 0)
    lane = lax.broadcasted_iota(jnp.int32, (1, width), 1)
    local = jnp.zeros((groups, width), F32)
    mine = jnp.zeros((groups, width), F32)
    start = (me * rows).astype(F32)
    for k in range(owners):
        at, live = unpack_line(packets[k], width)
        at = at - start
        here = (at >= F32(0.0)) & (at < F32(rows)) & live
        mine = jnp.where(group == k, jnp.where(here, F32(1.0), F32(0.0)), mine)
        local = jnp.where(group == k, at, local)
    ranks = jnp.dot(mine.astype(BF16), strict_upper(width), preferred_element_type=F32)
    sizes = jnp.sum(mine, axis=1, keepdims=True)
    total = jnp.sum(mine)
    tail = block // 2
    tails = (total.astype(jnp.int32) - block + (tail - 1)) // tail
    mark = F32(1 << 16)
    code = local + F32(1.0) + jnp.where(lane >= width // 2, mark, F32(0.0))
    offsets = []
    spots = []
    running = jnp.zeros((1, 1), F32)
    for k in range(owners):
        offsets.append(running)
        spots.append(jnp.where(mine[k : k + 1] > F32(0.5), ranks[k : k + 1] + running, F32(-1.0)))
        running = running + sizes[k : k + 1]

    piece = packets[0].shape[1]
    above = jnp.zeros((8, piece), F32)
    below = jnp.zeros((8, piece), F32)
    for k in range(1, owners):
        other = packets[k][...].astype(F32)
        above = jnp.where((me ^ k) == me - 1, other, above)
        below = jnp.where((me ^ k) == me + 1, other, below)
    span = 16
    foot_at = 16 + span
    after_at = foot_at + span + 8
    for j in range(columns):
        lanes = slice(j * LANES, (j + 1) * LANES)
        near[j, 8:foot_at, :] = feat_ref[0 : span + 8, lanes].astype(F32)
        near[j, foot_at:after_at, :] = feat_ref[rows - span - 8 : rows, lanes].astype(F32)
        part = j * LANES // piece
        inner = slice(j * LANES - part * piece, (j + 1) * LANES - part * piece)
        for h in range(HALO):
            row = h * PIECES + part
            near[j, 8 - HALO + h : 9 - HALO + h, :] = above[row : row + 1, inner]
            near[j, after_at + h : after_at + h + 1, :] = below[row : row + 1, inner]
    for origin, place in ((8, 0), (foot_at + 8, rows - span)):

        def load(j, k, origin=origin):
            begin = origin - HALO + k
            return near[j, begin : begin + span, :]

        out = conv_rows(load, taps_ref, gain_ref, columns, 1.0 / channels)
        for j in range(columns):
            patched_ref[place : place + span, j * LANES : (j + 1) * LANES] = out[j]

    wide = 256

    def encode_block(base, size, store):
        spread = lax.broadcasted_iota(jnp.int32, (size, rows), 1).astype(F32)
        level = lax.broadcasted_iota(jnp.int32, (size, width), 0).astype(F32)
        slot = lax.broadcasted_iota(jnp.int32, (capacity, size), 0).astype(F32)
        column = lax.broadcasted_iota(jnp.int32, (capacity, size), 1).astype(F32)
        part = slice(0, size)
        found = jnp.zeros((size, width), F32)
        for k in range(owners):
            found = jnp.where(spots[k] - base == level, code[k : k + 1, :], found)
        found = jnp.sum(found, axis=1, keepdims=True)
        accepts = found >= mark
        index = found - jnp.where(accepts, mark, F32(0.0)) - F32(1.0)
        grab = jnp.where(spread == index, F32(1.0), F32(0.0)).astype(BF16)
        for j in range(channels // wide):
            lanes = slice(j * wide, (j + 1) * wide)
            lhs[part, lanes] = jnp.dot(grab, patched_ref[:, lanes], preferred_element_type=F32).astype(BF16)
            res[part, lanes] = jnp.dot(grab, feat_ref[:, lanes], preferred_element_type=F32).astype(BF16)
        for j in range(channels // wide):
            lanes = slice(j * wide, (j + 1) * wide)
            mixed = jnp.dot(lhs[part, :], w_ref[:, lanes], preferred_element_type=F32)
            enc[part, lanes] = (res[part, lanes].astype(F32) + gelu(mixed)).astype(BF16)
        for j in range(heads // wide):
            lanes = slice(j * wide, (j + 1) * wide)
            left = jnp.dot(enc[part, :], wd_ref[:, lanes], preferred_element_type=F32)
            right = jnp.dot(enc[part, :], wa_ref[:, lanes], preferred_element_type=F32)
            proj[part, lanes] = jnp.where(accepts, right, left).astype(BF16)
        for k in range(owners):
            put = (column + base == offsets[k] + slot) & (slot < sizes[k : k + 1])
            put = jnp.where(put, F32(1.0), F32(0.0)).astype(BF16)
            store(outs[k], jnp.dot(put, proj[part, :], preferred_element_type=F32))

    def write(ref, value):
        ref[...] = value.astype(BF16)

    def add(ref, value):
        ref[...] = (ref[...].astype(F32) + value).astype(BF16)

    encode_block(F32(0.0), block, write)

    def body(c, carry):
        encode_block((block + c * tail).astype(F32), tail, add)
        return carry

    lax.fori_loop(0, tails, body, 0)


def named(packets, feat, normed, taps, gain, w, wd, wa, width, capacity):
    owners = len(packets)
    rows, channels = feat.shape
    heads = wd.shape[1]
    block = 128
    out = pl.pallas_call(
        functools.partial(named_kernel, owners, capacity, width),
        in_specs=[whole()] * (owners + 7),
        out_specs=[whole()] * (owners + 1),
        out_shape=[vmem((capacity, heads), BF16)] * owners + [vmem((rows, channels), BF16)],
        input_output_aliases={owners + 1: owners},
        scratch_shapes=[
            pltpu.VMEM((channels // LANES, 72, LANES), F32),
            pltpu.VMEM((block, channels), BF16),
            pltpu.VMEM((block, channels), BF16),
            pltpu.VMEM((block, channels), BF16),
            pltpu.VMEM((block, heads), BF16),
        ],
        compiler_params=params(16),
        cost_estimate=pl.CostEstimate(
            flops=8 * block * channels * (channels + rows), bytes_accessed=8 << 20, transcendentals=2 * block * channels
        ),
        name="named_rows",
    )(*packets, feat, normed, taps, gain.reshape(1, channels), w, wd, wa)
    return out[:owners], out[owners]


def encode_kernel(normed_ref, feat_ref, w_ref, out_hbm, stage, sem):
    rows, channels = feat_ref.shape
    wide = 256
    tall = 512
    copies = []
    tall = rows // 2
    for i in range(2):
        part = slice(i * tall, (i + 1) * tall)
        for j in range(channels // wide):
            lanes = slice(j * wide, (j + 1) * wide)
            mixed = jnp.dot(normed_ref[part, :], w_ref[:, lanes], preferred_element_type=F32)
            stage[part, lanes] = (feat_ref[part, lanes].astype(F32) + gelu(mixed)).astype(BF16)
            if j % 2 == 1:
                at = pl.ds((j - 1) * wide, 2 * wide)
                copy = pltpu.make_async_copy(
                    stage.at[pl.ds(i * tall, tall), at], out_hbm.at[pl.ds(i * tall, tall), at], sem.at[i * 3 + j // 2]
                )
                copy.start()
                copies.append(copy)
    for copy in copies:
        copy.wait()


def encode(normed, feat, w):
    rows, channels = feat.shape
    return pl.pallas_call(
        encode_kernel,
        in_specs=[whole()] * 3,
        out_specs=pl.BlockSpec(memory_space=pltpu.MemorySpace.HBM),
        out_shape=jax.ShapeDtypeStruct((rows, channels), BF16),
        scratch_shapes=[pltpu.VMEM((rows, channels), BF16), pltpu.SemaphoreType.DMA((channels // 256,))],
        compiler_params=params(6),
        cost_estimate=pl.CostEstimate(
            flops=2 * rows * channels * channels, bytes_accessed=8 << 20, transcendentals=2 * rows * channels
        ),
        name="encode",
    )(normed, feat, w)


def junction_kernel(owners, *refs):
    blocks = refs[:owners]
    spread_ref, out_hbm, stage, sem = refs[owners:]
    slots, heads = out_hbm.shape
    wide = 256
    copies = []
    for j in range(heads // wide):
        lanes = slice(j * wide, (j + 1) * wide)
        picked = lax.dot_general(
            spread_ref[...],
            jnp.concatenate([block[:, lanes] for block in blocks], axis=0),
            (((0,), (0,)), ((), ())),
            preferred_element_type=F32,
        )
        left, right = picked[:slots], picked[slots:]
        silu = left / (F32(1.0) + jnp.exp(-left))
        stage[:, lanes] = (silu * right).astype(BF16)
        at = pl.ds(j * wide, wide)
        copy = pltpu.make_async_copy(stage.at[:, at], out_hbm.at[:, at], sem.at[j])
        copy.start()
        copies.append(copy)
    for copy in copies:
        copy.wait()


def junction(blocks, spread):
    slots = spread.shape[1] // 2
    heads = blocks[0].shape[1]
    return pl.pallas_call(
        functools.partial(junction_kernel, len(blocks)),
        in_specs=[whole()] * (len(blocks) + 1),
        out_specs=in_hbm(),
        out_shape=jax.ShapeDtypeStruct((slots, heads), BF16),
        scratch_shapes=[pltpu.VMEM((slots, heads), BF16), pltpu.SemaphoreType.DMA((heads // 256,))],
        compiler_params=params(6),
        name="junction",
    )(*blocks, spread)


def swap_all(arrays):
    owners = len(arrays)
    got = [arrays[0]]
    for k in range(1, owners):
        got.append(lax.ppermute(arrays[k], "seq", [(i, i ^ k) for i in range(owners)]))
    return got


def on_device(
    features,
    conv_taps,
    norm_gain,
    point_weight,
    donor_weight,
    accept_weight,
    donor_pos,
    accept_pos,
    pair_counts,
):
    slots = donor_pos.shape[0]
    owners = lax.axis_size("seq")
    capacity = 2 * ((2 * slots + owners - 1) // owners)
    own = pack(features, donor_pos, accept_pos, pair_counts, owners)
    packets = swap_all(own)
    width = 2 * slots
    normed, wa, spread = conv_norm(
        own[0], features, conv_taps, norm_gain, point_weight, donor_weight, accept_weight, owners, capacity, width
    )
    sends, patched = named(
        packets, features, normed, conv_taps, norm_gain, point_weight, donor_weight, wa, width, capacity
    )
    blocks = swap_all(sends)
    encoded = encode(patched, features, point_weight)
    return encoded, junction(blocks, spread)


def solution(mesh):
    placed = (
        P(("dp", "seq"), None),
        P(),
        P(),
        P(),
        P(),
        P(),
        P(("dp", "seq")),
        P(("dp", "seq")),
        P(("dp", "seq")),
    )

    return jax.shard_map(
        on_device,
        mesh=mesh,
        in_specs=placed,
        out_specs=(P(("dp", "seq"), None), P(("dp", "seq"), None)),
        check_vma=False,
    )
```
